32 devices in a mesh: pipe: 2 (over x), expert: 16 (over z, y, core).
Axes of the slice: x: 2, y: 2, z: 4, core: 2. Of those that a mesh axis runs over, the one named last changes fastest.
Arguments:
- tokens: bfloat16 [2, 2048, 7168], P('pipe', 'expert'), may hold values from -24 to 24
- grad_out: bfloat16 [2, 2048, 7168], P('pipe', 'expert'), may hold values from -6 to 6
- norm_gain: float32 [2, 7168], P('pipe'), may hold values from 0.25 to 1.75
- expert_ids: int32 [2, 2048, 2], P('pipe', 'expert'), may hold values from 0 to 3, all different within a row; in each aligned block of 128 rows (0 to 127, 128 to 255, ..., all dimensions but the last counted through in order) at most 80 rows name the same one
- gate_weights: float32 [2, 2048, 2], P('pipe', 'expert'), may hold values from 0.2 to 1
- w_gate: bfloat16 [2, 7168, 4096], P('pipe', None, 'expert'), may hold values from -0.0625 to 0.0625
- w_up: bfloat16 [2, 7168, 4096], P('pipe', None, 'expert'), may hold values from -0.0625 to 0.0625
- w_down: bfloat16 [2, 4096, 7168], P('pipe', 'expert'), may hold values from -0.1875 to 0.1875
Outputs:
- next_in: bfloat16 [2, 2048, 7168], P('pipe', 'expert')
- prev_grad: bfloat16 [2, 2048, 7168], P('pipe', 'expert')
The draws below stay inside these ranges and needn't reach their ends.
Inputs may be any that keep to these rules, and one draw needn't show every extreme that they name: `expert_ids`: each token's 2 ids differ. In the rows of one device (aligned blocks of 128 rows of each section) no expert is named by more than 80 rows.
All inputs are finite; a program needn't handle non-finite values.
Results may differ from the reference program's by a relative error of at most 0.0048.
Values may be sent and summed in bfloat16 or wider, within the bound.
A program may use at most 192 MiB of HBM per device.

```python
import math
import jax
import jax.numpy as jnp
import numpy as np
from jax import lax

D = 7168
EH = 1024
SLICES = 4
TOP = 2
TOK_DEV = 128
FFD = 256
EXPERTS = 4
TOKENS = 2048
CAP = 80
N_PIPE = 2
N_EXPERT = 16


def draw_tokens(key, part):
    base_key = jax.random.fold_in(key, 11)
    keys = jax.random.split(base_key, 3)
    column_scale = jnp.exp(jax.random.uniform(keys[1], (1, 1, D), jnp.float32, math.log(0.3), math.log(3.0)))
    row_scale = jnp.exp(jax.random.uniform(keys[2], (N_PIPE, TOKENS, 1), jnp.float32, math.log(0.5), math.log(2.0)))
    base = jnp.clip(jax.random.normal(keys[0], (N_PIPE, TOKENS, D), jnp.float32), -4.0, 4.0)
    return (base * column_scale * row_scale).astype(jnp.bfloat16)


def shard_levels(stream_key, extent, cuts, low, top_value):
    def one(position, shards_of):
        heights = jax.random.uniform(jax.random.fold_in(jax.random.fold_in(stream_key, 6), position), (shards_of,), jnp.float32, low / len(cuts), top_value / len(cuts))
        return jnp.repeat(jnp.exp(heights), extent[position] // shards_of).reshape((-1,) + (1,) * (len(extent) - position - 1))

    factor_of = one(*cuts[0])
    for cut in cuts[1:]:
        factor_of = factor_of * one(*cut)
    return factor_of


def shared_out(key, own, number, rows, number_of, top, most, lean):
    sequence = jax.random.permutation(key, number_of)
    packed, ordinary = load_shares(number_of, rows * top, most, lean, True), load_shares(number_of, rows * top, most, lean, False)
    places = jnp.arange(number_of)

    def named(tallies, rotation):
        used = int((tallies > 0).sum())
        fixed = max(1, used // 4)
        moved = fixed + (places - fixed + rotation * (used - fixed)) % max(1, number_of - fixed)
        return jnp.zeros((number_of,), jnp.int32).at[sequence[jnp.where(places < fixed, places, moved)]].set(jnp.asarray(tallies, jnp.int32))

    tallies = jnp.where(number % 4 == 0, named(packed, number // 4), named(ordinary, number - number // 4 - 1))
    mixed = jax.random.permutation(jax.random.fold_in(own, 3), number_of)
    donor, sink = mixed[0:number_of // 2 * 2:2], mixed[1:number_of // 2 * 2:2]
    slack = jnp.minimum(tallies[donor] - 1, most - tallies[sink]) // 2
    slack = jnp.where((donor == sequence[0]) | (sink == sequence[0]) | (tallies[sink] == 0), 0, jnp.maximum(slack, 0))
    moved = jax.random.randint(jax.random.fold_in(own, 4), (number_of // 2,), 0, 1 << 20) % (slack + 1)
    tallies = tallies.at[donor].add(-moved).at[sink].add(moved)
    labels = jnp.searchsorted(jnp.cumsum(tallies), jnp.arange(rows * top), side="right").astype(jnp.int32)
    table = labels.reshape(top, rows).T
    table = table[jax.random.permutation(jax.random.fold_in(own, 1), rows)]
    rotation = jax.random.randint(jax.random.fold_in(own, 2), (rows, 1), 0, top)
    return jnp.take_along_axis(table, (jnp.arange(top)[None, :] + rotation) % top, axis=1)


def load_shares(count, total, reach, skew, full):
    weights = [(1 << 20) // math.isqrt(grade ** skew) + 1 for grade in range(1, count + 1)]
    largest = reach if full else min(reach, max(-(-total // count), total * weights[0] // sum(weights)))
    least = 1 if total - largest >= count - 1 else 0
    holding, surplus = [largest] + [least] * (count - 1), total - largest - least * (count - 1)
    while surplus > 0:
        candidates = [i for i in range(1, count) if holding[i] < largest] or [i for i in range(1, count) if holding[i] < reach]
        pool, left = sum([weights[i] for i in candidates]), surplus
        for i in candidates:
            extra = min(reach - holding[i], max(1, left * weights[i] // pool), surplus)
            holding[i] = holding[i] + extra
            surplus = surplus - extra
    return np.array(holding)


def noise(rng, extent, deviation, limit, pieces=(), kind=jnp.bfloat16):
    entries = jax.random.normal(rng, extent, jnp.float32) * deviation
    if len(pieces) > 0:
        entries = shard_levels(rng, extent, pieces, -0.22, 0.18) * entries
    return jnp.clip(entries, min=-limit, max=limit).astype(kind)


def setup_inputs(seed: int = 0) -> dict:
    key_list = jax.random.split(jax.random.key(seed), 9)
    tokens = draw_tokens(jax.random.fold_in(key_list[8], 71), 0)
    grad_out = noise(key_list[1], (N_PIPE, TOKENS, D), 1.0, 6.0, ((0, 2), (1, 16)))
    norm_gain = jnp.clip(1.0 + 0.15 * jax.random.normal(key_list[2], (N_PIPE, D), jnp.float32), 0.25, 1.75)
    expert_ids_keys = jax.random.split(jax.random.fold_in(key_list[3], 1), N_PIPE * TOKENS // TOK_DEV)
    expert_ids_turns = jax.random.permutation(jax.random.fold_in(key_list[3], 3), N_PIPE * TOKENS // TOK_DEV)
    expert_ids = jax.vmap(lambda own, number: shared_out(jax.random.fold_in(key_list[3], 2), own, number, TOK_DEV, EXPERTS, TOP, CAP, 2))(expert_ids_keys, expert_ids_turns).reshape((N_PIPE, TOKENS, TOP))
    gate_weights = jnp.clip(jnp.exp(math.log(1.0) - 1.609438 * jax.random.uniform(key_list[4], (N_PIPE, TOKENS, TOP), jnp.float32) ** shard_levels(key_list[4], (N_PIPE, TOKENS, TOP), ((0, 2), (1, 16)), -0.2, 0.2)), 0.2, 1.0)
    w_gate = noise(key_list[5], (N_PIPE, D, EXPERTS * EH), D ** -0.5, 0.0625, ((0, 2), (2, 16)))
    w_up = noise(key_list[6], (N_PIPE, D, EXPERTS * EH), D ** -0.5, 0.0625, ((0, 2), (2, 16)))
    w_down = noise(key_list[7], (N_PIPE, EXPERTS * EH, D), EH ** -0.5, 0.1875, ((0, 2), (1, 16)))
    return {"tokens": tokens, "grad_out": grad_out, "norm_gain": norm_gain, "expert_ids": expert_ids, "gate_weights": gate_weights, "w_gate": w_gate, "w_up": w_up, "w_down": w_down}


EPSILON = 1e-06

def transpose_dot(left_arr, right_arr):
    return lax.dot_general(left_arr, right_arr, (((1,), (1,)), ((), ())), preferred_element_type=jnp.float32)

def expert_apply(rows_in, rows_grad, gate_cols, up_cols, down_rows):
    gate_pre = jnp.dot(rows_in, gate_cols, preferred_element_type=jnp.float32)
    up_pre = jnp.dot(rows_in, up_cols, preferred_element_type=jnp.float32)
    sigmoid_gate = jax.nn.sigmoid(gate_pre)
    swish_gate = gate_pre * sigmoid_gate
    hidden = (swish_gate * up_pre).astype(jnp.bfloat16)
    part_out = jnp.dot(hidden, down_rows, preferred_element_type=jnp.float32).astype(jnp.bfloat16)
    grad_hidden = transpose_dot(rows_grad, down_rows)
    grad_gate = (grad_hidden * up_pre * sigmoid_gate * (1.0 + gate_pre * (1.0 - sigmoid_gate))).astype(jnp.bfloat16)
    grad_up = (grad_hidden * swish_gate).astype(jnp.bfloat16)
    part_grad = (transpose_dot(grad_gate, gate_cols) + transpose_dot(grad_up, up_cols)).astype(jnp.bfloat16)
    return (part_out, part_grad)

def section_layer(tokens, grad_out, gain_row, route_ids, route_weights, gate_all, up_all, down_all):
    token_count = tokens.shape[0]
    values = tokens.astype(jnp.float32)
    inverse = lax.rsqrt(lax.optimization_barrier(jnp.mean(values * values, axis=-1, keepdims=True)) + EPSILON)
    gain_wide = gain_row.astype(jnp.float32)[None, :]
    normed = (values * inverse * gain_wide).astype(jnp.bfloat16)
    flat_ids = route_ids.reshape(-1).astype(jnp.int32)
    pair_count = flat_ids.shape[0]
    sorted_pairs = jnp.argsort(flat_ids, stable=True).astype(jnp.int32)
    counts = lax.optimization_barrier(jnp.sum((flat_ids[:, None] == jnp.arange(EXPERTS, dtype=jnp.int32)[None, :]).astype(jnp.int32), axis=0))
    starts = (jnp.cumsum(counts) - counts).astype(jnp.int32)
    most_rows = N_EXPERT * CAP
    padded_pairs = jnp.concatenate([sorted_pairs, jnp.full((most_rows,), pair_count, jnp.int32)])
    normed_pad = jnp.concatenate([normed, jnp.zeros((1, D), jnp.bfloat16)])
    grad_pad = jnp.concatenate([grad_out, jnp.zeros((1, D), jnp.bfloat16)])

    def one_expert(expert_index):
        picked = lax.dynamic_slice_in_dim(padded_pairs, starts[expert_index], most_rows)
        live_rows = jnp.arange(most_rows, dtype=jnp.int32) < counts[expert_index]
        picked = jnp.where(live_rows, picked, pair_count).astype(jnp.int32)
        row_token = (picked // TOP).astype(jnp.int32)
        rows_in = normed_pad[row_token]
        rows_grad = grad_pad[row_token]
        sum_out = jnp.zeros((most_rows, D), jnp.float32)
        sum_grad = jnp.zeros((most_rows, D), jnp.float32)
        for slice_index in range(SLICES):
            column = (expert_index * EH + slice_index * FFD).astype(jnp.int32)
            gate_cols = lax.dynamic_slice_in_dim(gate_all, column, FFD, 1)
            up_cols = lax.dynamic_slice_in_dim(up_all, column, FFD, 1)
            down_rows = lax.dynamic_slice_in_dim(down_all, column, FFD, 0)
            part_out, part_grad = expert_apply(rows_in, rows_grad, gate_cols, up_cols, down_rows)
            sum_out = sum_out + part_out.astype(jnp.float32)
            sum_grad = sum_grad + part_grad.astype(jnp.float32)
        return (picked, sum_out, sum_grad)
    picked, outs, grads = lax.map(one_expert, jnp.arange(EXPERTS, dtype=jnp.int32))
    flat_pick = picked.reshape(-1)
    pair_out = jnp.zeros((pair_count + 1, D), jnp.float32).at[flat_pick].add(outs.reshape(-1, D))
    pair_grad = jnp.zeros((pair_count + 1, D), jnp.float32).at[flat_pick].add(grads.reshape(-1, D))
    weights = route_weights.astype(jnp.float32)[:, :, None]
    mixed_rows = lax.optimization_barrier(jnp.sum(pair_out[:pair_count].reshape(token_count, TOP, D) * weights, axis=1))
    grad_normed = lax.optimization_barrier(jnp.sum(pair_grad[:pair_count].reshape(token_count, TOP, D) * weights, axis=1))
    layer_out = (values + mixed_rows).astype(jnp.bfloat16)
    scaled = grad_normed * gain_wide
    cubed = inverse * inverse * inverse
    grad_in = (grad_out.astype(jnp.float32) + inverse * scaled - values * cubed * lax.optimization_barrier(jnp.mean(scaled * values, axis=-1, keepdims=True))).astype(jnp.bfloat16)
    return (layer_out, grad_in)

def reference(tokens, grad_out, norm_gain, expert_ids, gate_weights, w_gate, w_up, w_down):
    outputs = []
    gradients = []
    for section in range(N_PIPE):
        layer_out, grad_in = section_layer(tokens[section], grad_out[section], norm_gain[section], expert_ids[section], gate_weights[section], w_gate[section], w_up[section], w_down[section])
        outputs.append(layer_out)
        gradients.append(grad_in)
    stacked_out = jnp.stack(outputs)
    stacked_grad = jnp.stack(gradients)
    return (jnp.roll(stacked_out, 1, axis=0), jnp.roll(stacked_grad, -1, axis=0))
```

```python
import jax
import jax.numpy as jnp
from jax import lax
from jax.experimental import pallas as pl
from jax.experimental.pallas import tpu as pltpu
from jax.sharding import PartitionSpec as P

SLICES = 4
EPSILON = 1e-06
BF16 = jnp.bfloat16
F32 = jnp.float32


def move(value, pipe_steps, expert_map):
    pipes, devices = lax.axis_size("pipe"), lax.axis_size("expert")
    pairs = [
        (p * devices + d, ((p + pipe_steps) % pipes) * devices + expert_map(d))
        for p in range(pipes)
        for d in range(devices)
    ]
    return lax.ppermute(value, ("pipe", "expert"), pairs)


def dot_nt(left_arr, right_arr):
    return lax.dot_general(
        left_arr, right_arr, (((1,), (1,)), ((), ())), preferred_element_type=F32
    )


def dot_nn(left_arr, right_arr):
    return jnp.dot(left_arr, right_arr, preferred_element_type=F32)


def tile_of(width):
    for tile in (1024, 512, 256, 128):
        if width % tile == 0:
            return tile
    return width


def out_rows(hidden, downs, blocks, first, width):
    rows, ffd = hidden.shape[0], downs[0].shape[0]
    capacity = rows // blocks
    tile = tile_of(width)
    base = first // tile

    def kernel(h_ref, *refs):
        down_refs, out_refs = refs[:SLICES], refs[SLICES:]
        total = dot_nn(h_ref[:, 0:ffd], down_refs[0][...])
        for j in range(1, SLICES):
            total += dot_nn(h_ref[:, j * ffd : (j + 1) * ffd], down_refs[j][...])
        for s in range(blocks):
            out_refs[s][...] = total[s * capacity : (s + 1) * capacity].astype(BF16)

    return pl.pallas_call(
        kernel,
        grid=(width // tile,),
        in_specs=[pl.BlockSpec((rows, SLICES * ffd), lambda i: (0, 0))]
        + [pl.BlockSpec((ffd, tile), lambda i: (0, i + base))] * SLICES,
        out_specs=[pl.BlockSpec((capacity, tile), lambda i: (0, i))] * blocks,
        out_shape=[jax.ShapeDtypeStruct((capacity, width), BF16)] * blocks,
        compiler_params=pltpu.CompilerParams(vmem_limit_bytes=40 * 1024 * 1024),
        cost_estimate=pl.CostEstimate(
            flops=2 * rows * SLICES * ffd * width,
            bytes_accessed=2 * width * (SLICES * ffd + rows),
            transcendentals=0,
        ),
        name="out_rows",
    )(hidden, *downs)


def grad_rows_back(grad_gate, grad_up, gates, ups, blocks, first, width):
    rows, ffd = grad_gate.shape[0], gates[0].shape[1]
    capacity = rows // blocks
    tile = tile_of(width)
    base = first // tile

    def kernel(g_ref, u_ref, *refs):
        gate_refs, up_refs, out_refs = refs[:SLICES], refs[SLICES : 2 * SLICES], refs[2 * SLICES :]
        total = None
        for j in range(SLICES):
            cols = slice(j * ffd, (j + 1) * ffd)
            part = dot_nt(g_ref[:, cols], gate_refs[j][...]) + dot_nt(u_ref[:, cols], up_refs[j][...])
            total = part if total is None else total + part
        for s in range(blocks):
            out_refs[s][...] = total[s * capacity : (s + 1) * capacity].astype(BF16)

    return pl.pallas_call(
        kernel,
        grid=(width // tile,),
        in_specs=[pl.BlockSpec((rows, SLICES * ffd), lambda i: (0, 0))] * 2
        + [pl.BlockSpec((tile, ffd), lambda i: (i + base, 0))] * (2 * SLICES),
        out_specs=[pl.BlockSpec((capacity, tile), lambda i: (0, i))] * blocks,
        out_shape=[jax.ShapeDtypeStruct((capacity, width), BF16)] * blocks,
        compiler_params=pltpu.CompilerParams(vmem_limit_bytes=40 * 1024 * 1024),
        cost_estimate=pl.CostEstimate(
            flops=4 * rows * SLICES * ffd * width,
            bytes_accessed=2 * width * (2 * SLICES * ffd + rows),
            transcendentals=0,
        ),
        name="grad_rows",
    )(grad_gate, grad_up, *gates, *ups)


def slots_of(route_ids, home, experts, capacity):
    token_count, top_count = route_ids.shape
    relative = (route_ids.reshape(-1) - home + experts) % experts
    onehot = (relative[:, None] == jnp.arange(experts, dtype=jnp.int32)[None, :]).astype(jnp.int32)
    before = jnp.cumsum(onehot, axis=0) - onehot
    target = relative * capacity + jnp.sum(before * onehot, axis=1)
    return target.reshape(token_count, top_count)


def gather_slices(weight):
    far = move(weight, 0, lambda d: d ^ 2)
    near = move(weight, 0, lambda d: d ^ 1)
    cross = move(far, 0, lambda d: d ^ 1)
    return [weight, near, far, cross]


def pick_back(pair_slot, weights, back, experts, capacity):
    slots = jnp.arange(experts * capacity, dtype=jnp.int32)[None, :]
    rows = jnp.concatenate(back, axis=0)
    total = None
    for k in range(pair_slot.shape[1]):
        picker = (pair_slot[:, k : k + 1] == slots).astype(BF16)
        part = dot_nn(picker, rows) * weights[:, k : k + 1]
        total = part if total is None else total + part
    return total


def inverse_of(values):
    return lax.rsqrt(jnp.mean(values * values, axis=-1, keepdims=True) + EPSILON)


def body(tokens, grad_out, norm_gain, expert_ids, gate_weights, w_gate, w_up, w_down):
    tokens = tokens[0]
    grad_rows = grad_out[0]
    gain = norm_gain[0][None, :]
    route_ids = expert_ids[0]
    route_weights = gate_weights[0]
    token_count, width = tokens.shape
    top_count = route_ids.shape[1]
    devices = lax.axis_size("expert")
    pipes = lax.axis_size("pipe")
    experts = devices // SLICES
    step_size = 4 * experts * SLICES
    capacity = min(
        token_count, SLICES * ((token_count * top_count * 5 + step_size - 1) // step_size)
    )
    home = lax.axis_index("expert") // SLICES
    same = lambda d: d

    gates, ups, downs = gather_slices(w_gate[0]), gather_slices(w_up[0]), gather_slices(w_down[0])

    routing = jnp.concatenate([route_ids.astype(F32), route_weights], axis=1)
    routing_next = move(routing, 1, same)
    tokens_next = move(tokens, 1, same)
    if pipes == 2:
        routing_prev, tokens_prev = routing_next, tokens_next
    else:
        routing_prev = move(routing, -1, same)
        tokens_prev = move(tokens, -1, same)
    grad_prev = move(grad_rows, -1, same)
    gain_prev = move(gain, -1, same)

    values = tokens.astype(F32)
    normed = (values * inverse_of(values) * gain).astype(BF16)
    pair_slot = slots_of(route_ids, home, experts, capacity)
    pickers = [
        jnp.any(
            pair_slot[None, :, :]
            == (s * capacity + jnp.arange(capacity, dtype=jnp.int32))[:, None, None],
            axis=2,
        ).astype(BF16)
        for s in range(experts)
    ]

    def dispatch(rows):
        blocks = []
        for s in range(experts):
            block = dot_nn(pickers[s], rows).astype(BF16)
            if s:
                block = move(block, 0, lambda d, s=s: (d + SLICES * s) % devices)
            blocks.append(block)
        return jnp.concatenate(blocks, axis=0)

    rows_in = dispatch(normed)
    rows_back = dispatch(grad_rows)

    hidden, gates_grad, ups_grad = [], [], []
    for j in range(SLICES):
        gate_pre = dot_nn(rows_in, gates[j])
        up_pre = dot_nn(rows_in, ups[j])
        sig = jax.nn.sigmoid(gate_pre)
        swish = gate_pre * sig
        hidden.append((swish * up_pre).astype(BF16))
        grad_hidden = dot_nt(rows_back, downs[j])
        gates_grad.append((grad_hidden * up_pre * sig * (1.0 + gate_pre * (1.0 - sig))).astype(BF16))
        ups_grad.append((grad_hidden * swish).astype(BF16))
    hidden = jnp.concatenate(hidden, axis=1)
    gates_grad = jnp.concatenate(gates_grad, axis=1)
    ups_grad = jnp.concatenate(ups_grad, axis=1)

    def send_back(blocks, pipe_steps):
        return [
            move(block, pipe_steps, lambda d, s=s: (d - SLICES * s) % devices)
            for s, block in enumerate(blocks)
        ]

    back_out = send_back(out_rows(hidden, downs, experts, 0, width), 1)
    back_grad = send_back(grad_rows_back(gates_grad, ups_grad, gates, ups, experts, 0, width), -1)

    def routing_of(table):
        ids = table[:, :top_count].astype(jnp.int32)
        return slots_of(ids, home, experts, capacity), table[:, top_count:]

    slot_next, weights_next = routing_of(routing_next)
    slot_prev, weights_prev = routing_of(routing_prev)
    mixed = pick_back(slot_next, weights_next, back_out, experts, capacity)
    next_rows = (tokens_next.astype(F32) + mixed).astype(BF16)

    scaled = pick_back(slot_prev, weights_prev, back_grad, experts, capacity) * gain_prev
    values_prev = tokens_prev.astype(F32)
    inverse = inverse_of(values_prev)
    cubed = inverse * inverse * inverse
    prev_rows = (
        grad_prev.astype(F32)
        + inverse * scaled
        - values_prev * cubed * jnp.mean(scaled * values_prev, axis=-1, keepdims=True)
    ).astype(BF16)
    return (next_rows[None], prev_rows[None])


def solution(mesh):
    return jax.shard_map(
        body,
        mesh=mesh,
        in_specs=(
            P("pipe", "expert", None),
            P("pipe", "expert", None),
            P("pipe", None),
            P("pipe", "expert", None),
            P("pipe", "expert", None),
            P("pipe", None, "expert"),
            P("pipe", None, "expert"),
            P("pipe", "expert", None),
        ),
        out_specs=(P("pipe", "expert", None), P("pipe", "expert", None)),
        check_vma=False,
    )
```

```python
import jax
import jax.numpy as jnp
from jax import lax
from jax.experimental import pallas as pl
from jax.experimental.pallas import tpu as pltpu
from jax.sharding import PartitionSpec as P

SLICES = 4
EPSILON = 1e-06
BF16 = jnp.bfloat16
F32 = jnp.float32


def move(value, pipe_steps, expert_map):
    pipes, devices = lax.axis_size("pipe"), lax.axis_size("expert")
    pairs = [
        (p * devices + d, ((p + pipe_steps) % pipes) * devices + expert_map(d))
        for p in range(pipes)
        for d in range(devices)
    ]
    return lax.ppermute(value, ("pipe", "expert"), pairs)


def dot_nt(left_arr, right_arr):
    return lax.dot_general(
        left_arr, right_arr, (((1,), (1,)), ((), ())), preferred_element_type=F32
    )


def dot_nn(left_arr, right_arr):
    return jnp.dot(left_arr, right_arr, preferred_element_type=F32)


def tile_of(width):
    for tile in (1024, 512, 256, 128):
        if width % tile == 0:
            return tile
    return width


MESH = pl.DeviceIdType.MESH
ANY = pl.BlockSpec(memory_space=pl.ANY)


def sections():
    pipe, pipes = lax.axis_index("pipe"), lax.axis_size("pipe")
    return pipe, lax.rem(pipe + 1, pipes), lax.rem(pipe + pipes - 1, pipes)


def greet(partners):
    barrier = pltpu.get_barrier_semaphore()
    for partner in partners:
        pl.semaphore_signal(barrier, inc=1, device_id=partner, device_id_type=MESH)
    pl.semaphore_wait(barrier, len(partners))


def gather_all(slots_in, slots_grad, gate, up, down, tokens, grad_rows):
    experts = slots_in.shape[0]
    devices, pipes = lax.axis_size("expert"), lax.axis_size("pipe")
    two = pipes == 2

    def kernel(si, sg, wg, wu, wd, tok, grd, ri, rg, ag, au, ad, tn, tp, gp, send, recv, local):
        pipe, after, ahead = sections()
        me = lax.axis_index("expert")
        place = lax.rem(me, SLICES)
        base = me - place
        far = base + lax.rem(place + 2, SLICES)
        near = me + 1 - 2 * lax.rem(me, 2)
        others = [(pipe, lax.rem(me + SLICES * s, devices)) for s in range(1, experts)]
        greet(others + [(pipe, far), (pipe, near), (after, me), (ahead, me)])
        count = [0]

        def push(source, target, device):
            n = count[0]
            count[0] += 1
            copy = pltpu.make_async_remote_copy(
                src_ref=source,
                dst_ref=target,
                send_sem=send.at[n],
                recv_sem=recv.at[n],
                device_id=device,
                device_id_type=MESH,
            )
            copy.start()
            return copy

        pairs = [(wg, ag), (wu, au), (wd, ad)]
        fars = [push(w, all_w.at[1], (pipe, far)) for w, all_w in pairs]
        copies = []
        for source, target in ((si, ri), (sg, rg)):
            for s in range(experts - 1, 0, -1):
                copies.append(push(source.at[s], target.at[s], others[s - 1]))
        own = [
            pltpu.make_async_copy(source.at[0], target.at[0], local.at[n])
            for n, (source, target) in enumerate(((si, ri), (sg, rg)))
        ]
        for copy in own:
            copy.start()
        copies += [push(w, all_w.at[0], (pipe, near)) for w, all_w in pairs]
        copies.append(push(tok, tn, (after, me)))
        if not two:
            copies.append(push(tok, tp, (ahead, me)))
        copies.append(push(grd, gp, (ahead, me)))
        for first, (w, all_w) in zip(fars, pairs):
            first.wait()
            copies.append(push(all_w.at[1], all_w.at[2], (pipe, near)))
        for copy in own + copies:
            copy.wait()

    like = lambda value: jax.ShapeDtypeStruct(value.shape, value.dtype)
    three = lambda value: jax.ShapeDtypeStruct((3,) + value.shape, value.dtype)
    total = 2 * (experts - 1) + 9 + (2 if two else 3)
    inputs = (slots_in, slots_grad, gate, up, down, tokens, grad_rows)
    small = jax.ShapeDtypeStruct((16, 128), tokens.dtype)
    outs = pl.pallas_call(
        kernel,
        in_specs=[ANY] * 7,
        out_specs=[ANY] * 8,
        out_shape=[like(slots_in), like(slots_grad), three(gate), three(up), three(down)]
        + [like(tokens), small if two else like(tokens), like(grad_rows)],
        scratch_shapes=[
            pltpu.SemaphoreType.DMA((total,)),
            pltpu.SemaphoreType.DMA((total,)),
            pltpu.SemaphoreType.DMA((2,)),
        ],
        compiler_params=pltpu.CompilerParams(
            collective_id=0, has_side_effects=True, vmem_limit_bytes=VMEM
        ),
        name="gather_all",
    )(*inputs)
    outs = list(outs)
    if two:
        outs[6] = outs[5]
    return outs


VMEM = 58 * 1024 * 1024


def results(hidden, gates_grad, ups_grad, gate, up, down, all_gate, all_up, all_down,
            tok_next, tok_prev, grad_prev, gain_prev, inverse_prev,
            pick_next, wt_next, pick_prev, wt_prev):
    rows, ffd = hidden.shape[0], down.shape[0]
    width = down.shape[1]
    experts, _, capacity = pick_next.shape
    token_count, top = wt_next.shape
    devices = lax.axis_size("expert")
    tile = tile_of(width)
    tiles = width // tile

    def kernel(h, gg, ug, wg, wu, wd, ag, au, ad, tn, tp, gp, gain, inv, pn, wn, pp, wp,
               next_ref, prev_ref, stage_o, stage_g, recv_o, recv_g, scaled, send, recv):
        step = pl.program_id(0)
        pipe, after, ahead = sections()
        me = lax.axis_index("expert")
        homes = [lax.rem(me + devices - SLICES * s, devices) for s in range(experts)]

        @pl.when(step == 0)
        def _():
            greet([(p, d) for p in (after, ahead) for d in homes])

        def cols_of(i):
            return pl.ds(pl.multiple_of(i * tile, tile), tile)

        def copy_of(which, i, s):
            stage, target = ((stage_o, recv_o), (stage_g, recv_g))[which]
            return pltpu.make_async_remote_copy(
                src_ref=stage.at[s, :, cols_of(i)],
                dst_ref=target.at[s, :, cols_of(i)],
                send_sem=send.at[which, i, s],
                recv_sem=recv.at[which, i, s],
                device_id=((after, ahead)[which], homes[s]),
                device_id_type=MESH,
            )

        def ship(which, total):
            stage = (stage_o, stage_g)[which]
            for s in range(experts):
                stage[s, :, cols_of(step)] = total[s * capacity : (s + 1) * capacity].astype(BF16)
            for s in range(experts):
                copy_of(which, step, s).start()

        total = dot_nn(h[:, 0:ffd], wd[...])
        for j in range(1, SLICES):
            total += dot_nn(h[:, j * ffd : (j + 1) * ffd], ad[j - 1])
        ship(0, total)
        total = dot_nt(gg[:, 0:ffd], wg[...]) + dot_nt(ug[:, 0:ffd], wu[...])
        for j in range(1, SLICES):
            part = slice(j * ffd, (j + 1) * ffd)
            total += dot_nt(gg[:, part], ag[j - 1]) + dot_nt(ug[:, part], au[j - 1])
        ship(1, total)

        @pl.when(step == tiles - 1)
        def _():
            def picked(target, pick, weights, cols):
                total = dot_nn(pick[0], target[0, :, cols])
                for s in range(1, experts):
                    total += dot_nn(pick[s], target[s, :, cols])
                value = total[:token_count] * weights[:, 0:1]
                for k in range(1, top):
                    value += total[k * token_count : (k + 1) * token_count] * weights[:, k : k + 1]
                return value

            def finish(i, mean):
                cols = cols_of(i)
                for s in range(experts):
                    copy_of(0, i, s).wait()
                mixed = picked(recv_o, pn, wn, cols)
                next_ref[:, cols] = (tn[:, cols].astype(F32) + mixed).astype(BF16)
                for s in range(experts):
                    copy_of(1, i, s).wait()
                part = picked(recv_g, pp, wp, cols) * gain[:, cols]
                scaled[:, cols] = part
                return mean + jnp.sum(part * tp[:, cols].astype(F32), axis=1, keepdims=True)

            mean = lax.fori_loop(0, tiles, finish, jnp.zeros((token_count, 1), F32)) / width
            inverse = inv[...]
            factor = inverse * inverse * inverse * mean

            def last(i, carry):
                cols = cols_of(i)
                prev_ref[:, cols] = (
                    gp[:, cols].astype(F32)
                    + inverse * scaled[:, cols]
                    - tp[:, cols].astype(F32) * factor
                ).astype(BF16)
                return carry

            lax.fori_loop(0, tiles, last, 0)

    def whole(value):
        return pl.BlockSpec(
            value.shape, lambda i, n=value.ndim: (0,) * n, pipeline_mode=pl.Buffered(1)
        )

    fixed = [tok_next, tok_prev, grad_prev, gain_prev, inverse_prev, pick_next, wt_next, pick_prev, wt_prev]
    in_specs = [whole(hidden), whole(gates_grad), whole(ups_grad)]
    in_specs += [pl.BlockSpec((tile, ffd), lambda i: (i, 0))] * 2
    in_specs += [pl.BlockSpec((ffd, tile), lambda i: (0, i))]
    in_specs += [pl.BlockSpec((3, tile, ffd), lambda i: (0, i, 0))] * 2
    in_specs += [pl.BlockSpec((3, ffd, tile), lambda i: (0, 0, i))]
    in_specs += [whole(value) for value in fixed]
    result = jax.ShapeDtypeStruct((token_count, width), BF16)
    rows_shape = (experts, capacity, width)
    return pl.pallas_call(
        kernel,
        grid=(tiles,),
        in_specs=in_specs,
        out_specs=[pl.BlockSpec((token_count, width), lambda i: (0, 0), pipeline_mode=pl.Buffered(1))] * 2,
        out_shape=[result] * 2,
        scratch_shapes=[pltpu.VMEM(rows_shape, BF16)] * 4
        + [pltpu.VMEM((token_count, width), F32)]
        + [pltpu.SemaphoreType.DMA((2, tiles, experts))] * 2,
        compiler_params=pltpu.CompilerParams(
            collective_id=1, has_side_effects=True, vmem_limit_bytes=VMEM
        ),
        name="results",
    )(hidden, gates_grad, ups_grad, gate, up, down, all_gate, all_up, all_down, *fixed)


def slots_of(route_ids, home, experts, capacity):
    token_count, top_count = route_ids.shape
    relative = (route_ids.reshape(-1) - home + experts) % experts
    onehot = (relative[:, None] == jnp.arange(experts, dtype=jnp.int32)[None, :]).astype(jnp.int32)
    before = jnp.cumsum(onehot, axis=0) - onehot
    target = relative * capacity + jnp.sum(before * onehot, axis=1)
    return target.reshape(token_count, top_count)


def pickers_of(pair_slot, experts, capacity):
    flat = pair_slot.T.reshape(-1)
    slots = jnp.arange(experts * capacity, dtype=jnp.int32).reshape(experts, 1, capacity)
    return (flat[None, :, None] == slots).astype(BF16)


def inverse_of(values):
    return lax.rsqrt(jnp.mean(values * values, axis=-1, keepdims=True) + EPSILON)


def body(tokens, grad_out, norm_gain, expert_ids, gate_weights, w_gate, w_up, w_down):
    tokens = tokens[0]
    grad_rows = grad_out[0]
    gain = norm_gain[0][None, :]
    route_ids = expert_ids[0]
    route_weights = gate_weights[0]
    token_count, width = tokens.shape
    top_count = route_ids.shape[1]
    devices = lax.axis_size("expert")
    pipes = lax.axis_size("pipe")
    experts = devices // SLICES
    step_size = 4 * experts * SLICES
    capacity = min(
        token_count, SLICES * ((token_count * top_count * 5 + step_size - 1) // step_size)
    )
    home = lax.axis_index("expert") // SLICES
    same = lambda d: d

    gate, up, down = w_gate[0], w_up[0], w_down[0]

    routing = jnp.concatenate([route_ids.astype(F32), route_weights], axis=1)
    routing_next = move(routing, 1, same)
    routing_prev = routing_next if pipes == 2 else move(routing, -1, same)
    gain_prev = move(gain, -1, same)

    values = tokens.astype(F32)
    normed = (values * inverse_of(values) * gain).astype(BF16)
    pair_slot = slots_of(route_ids, home, experts, capacity)
    picker = jnp.any(
        pair_slot[None, :, :]
        == jnp.arange(experts * capacity, dtype=jnp.int32)[:, None, None],
        axis=2,
    ).astype(BF16)

    def slotted(rows):
        return dot_nn(picker, rows).astype(BF16).reshape(experts, capacity, width)

    rows_in, rows_back, all_gate, all_up, all_down, tok_next, tok_prev, grad_prev = gather_all(
        slotted(normed), slotted(grad_rows), gate, up, down, tokens, grad_rows
    )
    rows_in = rows_in.reshape(experts * capacity, width)
    rows_back = rows_back.reshape(experts * capacity, width)

    hidden, gates_grad, ups_grad = [], [], []
    for j in range(SLICES):
        gate_cols, up_cols, down_rows = (
            (gate, up, down) if j == 0 else (all_gate[j - 1], all_up[j - 1], all_down[j - 1])
        )
        gate_pre = dot_nn(rows_in, gate_cols)
        up_pre = dot_nn(rows_in, up_cols)
        sig = jax.nn.sigmoid(gate_pre)
        swish = gate_pre * sig
        hidden.append((swish * up_pre).astype(BF16))
        grad_hidden = dot_nt(rows_back, down_rows)
        gates_grad.append((grad_hidden * up_pre * sig * (1.0 + gate_pre * (1.0 - sig))).astype(BF16))
        ups_grad.append((grad_hidden * swish).astype(BF16))
    hidden = jnp.concatenate(hidden, axis=1)
    gates_grad = jnp.concatenate(gates_grad, axis=1)
    ups_grad = jnp.concatenate(ups_grad, axis=1)

    def routing_of(table):
        ids = table[:, :top_count].astype(jnp.int32)
        slots = slots_of(ids, home, experts, capacity)
        return pickers_of(slots, experts, capacity), table[:, top_count:]

    pick_next, weights_next = routing_of(routing_next)
    pick_prev, weights_prev = routing_of(routing_prev)
    next_rows, prev_rows = results(
        hidden, gates_grad, ups_grad, gate, up, down, all_gate, all_up, all_down,
        tok_next, tok_prev, grad_prev, gain_prev, inverse_of(tok_prev.astype(F32)),
        pick_next, weights_next, pick_prev, weights_prev,
    )
    return (next_rows[None], prev_rows[None])


def solution(mesh):
    return jax.shard_map(
        body,
        mesh=mesh,
        in_specs=(
            P("pipe", "expert", None),
            P("pipe", "expert", None),
            P("pipe", None),
            P("pipe", "expert", None),
            P("pipe", "expert", None),
            P("pipe", None, "expert"),
            P("pipe", None, "expert"),
            P("pipe", "expert", None),
        ),
        out_specs=(P("pipe", "expert", None), P("pipe", "expert", None)),
        check_vma=False,
    )
```

```python
import jax
import jax.numpy as jnp
from jax import lax
from jax.experimental import pallas as pl
from jax.experimental.pallas import tpu as pltpu
from jax.sharding import PartitionSpec as P

SLICES = 4
EPSILON = 1e-06
BF16 = jnp.bfloat16
F32 = jnp.float32


def move(value, pipe_steps, expert_map):
    pipes, devices = lax.axis_size("pipe"), lax.axis_size("expert")
    pairs = [
        (p * devices + d, ((p + pipe_steps) % pipes) * devices + expert_map(d))
        for p in range(pipes)
        for d in range(devices)
    ]
    return lax.ppermute(value, ("pipe", "expert"), pairs)


def dot_nt(left_arr, right_arr):
    return lax.dot_general(
        left_arr, right_arr, (((1,), (1,)), ((), ())), preferred_element_type=F32
    )


def dot_nn(left_arr, right_arr):
    return jnp.dot(left_arr, right_arr, preferred_element_type=F32)


def tile_of(width):
    for tile in (1024, 512, 256, 128):
        if width % tile == 0:
            return tile
    return width


MESH = pl.DeviceIdType.MESH
ANY = pl.BlockSpec(memory_space=pl.ANY)


def sections():
    pipe, pipes = lax.axis_index("pipe"), lax.axis_size("pipe")
    return pipe, lax.rem(pipe + 1, pipes), lax.rem(pipe + pipes - 1, pipes)


def greet(partners):
    barrier = pltpu.get_barrier_semaphore()
    for partner in partners:
        pl.semaphore_signal(barrier, inc=1, device_id=partner, device_id_type=MESH)
    pl.semaphore_wait(barrier, len(partners))


VMEM = 60 * 1024 * 1024


def layer(slots_in, slots_grad, gate, up, down, tokens, grad_rows,
          gain_prev, inverse_prev, pick_next, wt_next, pick_prev, wt_prev):
    experts, capacity, width = slots_in.shape
    rows = experts * capacity
    ffd = down.shape[0]
    token_count, top = wt_next.shape
    devices, pipes = lax.axis_size("expert"), lax.axis_size("pipe")
    tile = tile_of(width)
    tiles = width // tile

    def kernel(si, sg, wg, wu, wd, tok, grd, gain, inv, pn, wn, pp, wp,
               next_ref, prev_ref, ag, au, ad,
               ri, rg, tn, tp, gp, recv_o, recv_g, scaled, acc_g, acc_u, acc_h, hid, gg, ug,
               buf_g, buf_u, buf_d,
               far_s, far_r, cross_s, cross_r, near_s, near_r, rows_s, rows_r, tok_s, tok_r,
               load_sem, own_sem, send, recv):
        pipe, after, ahead = sections()
        me = lax.axis_index("expert")
        place = lax.rem(me, SLICES)
        far = me - place + lax.rem(place + 2, SLICES)
        near = me + 1 - 2 * lax.rem(me, 2)
        others = [lax.rem(me + SLICES * s, devices) for s in range(1, experts)]
        homes = [lax.rem(me + devices - SLICES * s, devices) for s in range(experts)]
        greet(
            [(pipe, d) for d in others]
            + [(pipe, far), (pipe, near)]
            + [(p, d) for p in (after, ahead) for d in homes]
        )
        weights = ((wg, ag, buf_g), (wu, au, buf_u), (wd, ad, buf_d))
        stages = (ri, rg)

        def remote(source, target, send_sem, recv_sem, device):
            return pltpu.make_async_remote_copy(
                src_ref=source, dst_ref=target, send_sem=send_sem, recv_sem=recv_sem,
                device_id=device, device_id_type=MESH,
            )

        def cols_of(i):
            return pl.ds(pl.multiple_of(i * tile, tile), tile)

        def part(ref, which, i):
            return ref.at[cols_of(i), :] if which < 2 else ref.at[:, cols_of(i)]

        def far_copy(which, i):
            own, full, _ = weights[which]
            return remote(
                part(own, which, i), part(full.at[1], which, i),
                far_s.at[which, i], far_r.at[which, i], (pipe, far),
            )

        def cross_copy(which, i):
            full = weights[which][1]
            return remote(
                part(full.at[1], which, i), part(full.at[2], which, i),
                cross_s.at[which, i], cross_r.at[which, i], (pipe, near),
            )

        def near_copy(which):
            own, full, _ = weights[which]
            return remote(own, full.at[0], near_s.at[which], near_r.at[which], (pipe, near))

        def row_copy(which, i, s):
            return remote(
                (si, sg)[which].at[s, :, cols_of(i)], stages[which].at[s, :, cols_of(i)],
                rows_s.at[which, i, s - 1], rows_r.at[which, i, s - 1], (pipe, others[s - 1]),
            )

        def own_copy(which):
            return pltpu.make_async_copy((si, sg)[which].at[0], stages[which].at[0], own_sem.at[which])

        def token_copies():
            moves = [(tok, tn, after), (grd, gp, ahead), (tok, tp, ahead)]
            return [
                remote(source, target, tok_s.at[n], tok_r.at[n], (device, me))
                for n, (source, target, device) in enumerate(moves)
            ]

        def loads(which, i):
            own, full, buf = weights[which]
            slot = lax.rem(i, 2)
            return [
                pltpu.make_async_copy(
                    part(own if j == 0 else full.at[j - 1], which, i),
                    buf.at[slot, j],
                    load_sem.at[which, slot, j],
                )
                for j in range(SLICES)
            ]

        def load(kinds, i):
            for which in kinds:
                for copy in loads(which, i):
                    copy.start()

        def loaded(kinds, i):
            for which in kinds:
                for copy in loads(which, i):
                    copy.wait()

        def result_copy(which, i, s):
            return remote(
                stages[which].at[s, :, cols_of(i)], (recv_o, recv_g)[which].at[s, :, cols_of(i)],
                send.at[which, i, s], recv.at[which, i, s], ((after, ahead)[which], homes[s]),
            )

        def ship(which, i, total):
            for s in range(experts):
                stages[which][s, :, cols_of(i)] = total[s * capacity : (s + 1) * capacity].astype(BF16)
            for s in range(experts):
                result_copy(which, i, s).start()

        def send_rows(which, i):
            for s in range(experts - 1, 0, -1):
                row_copy(which, i, s).start()

        def send_far(kinds, i):
            for which in kinds:
                far_copy(which, i).start()

        def tile_rows(which, i):
            return stages[which][:, :, cols_of(i)].reshape(rows, tile)

        def piece(j):
            return slice(j * ffd, (j + 1) * ffd)

        first_far, first_down = min(2, tiles), min(4, tiles)
        for i in range(first_far):
            send_far((0, 1), i)

        @pl.loop(0, tiles)
        def _(i):
            send_rows(0, i)

        for which in range(3):
            near_copy(which).start()
        for which in range(2):
            own_copy(which).start()
        for copy in token_copies():
            copy.start()
        acc_g[...] = jnp.zeros_like(acc_g)
        acc_u[...] = jnp.zeros_like(acc_u)
        acc_h[...] = jnp.zeros_like(acc_h)
        near_copy(0).wait()
        near_copy(1).wait()
        own_copy(0).wait()

        def pipeline(kinds, arrive, compute):
            @pl.loop(0, tiles + 2)
            def _(i):
                @pl.when(i < tiles)
                def _():
                    arrive(i)
                    for which in kinds:
                        far_copy(which, i).wait()
                        cross_copy(which, i).start()

                @pl.when((i >= 1) & (i <= tiles))
                def _():
                    for which in kinds:
                        cross_copy(which, i - 1).wait()
                    load(kinds, i - 1)

                @pl.when(i >= 2)
                def _():
                    loaded(kinds, i - 2)
                    compute(i - 2)

        def arrive_first(i):
            send_rows(1, i)

            @pl.when(i + first_far < tiles)
            def _():
                send_far((0, 1), i + first_far)

            @pl.when(i == tiles - 1)
            def _():
                for n in range(first_down):
                    send_far((2,), n)

        def compute_first(i):
            for s in range(1, experts):
                row_copy(0, i, s).wait()
            slot = lax.rem(i, 2)
            block = tile_rows(0, i)
            for j in range(SLICES):
                acc_g[:, piece(j)] += dot_nn(block, buf_g[slot, j])
                acc_u[:, piece(j)] += dot_nn(block, buf_u[slot, j])

        pipeline((0, 1), arrive_first, compute_first)

        for j in range(SLICES):
            gate_pre = acc_g[:, piece(j)]
            hid[:, piece(j)] = (gate_pre * jax.nn.sigmoid(gate_pre) * acc_u[:, piece(j)]).astype(BF16)
        near_copy(2).wait()
        own_copy(1).wait()

        def arrive_down(i):
            @pl.when(i + first_down < tiles)
            def _():
                send_far((2,), i + first_down)

        def compute_down(i):
            slot = lax.rem(i, 2)
            total = dot_nn(hid[:, piece(0)], buf_d[slot, 0])
            for j in range(1, SLICES):
                total += dot_nn(hid[:, piece(j)], buf_d[slot, j])
            ship(0, i, total)
            for s in range(1, experts):
                row_copy(1, i, s).wait()
            block = tile_rows(1, i)
            for j in range(SLICES):
                acc_h[:, piece(j)] += dot_nt(block, buf_d[slot, j])

        pipeline((2,), arrive_down, compute_down)

        load((0, 1), 0)
        for j in range(SLICES):
            gate_pre, up_pre, grad_hidden = acc_g[:, piece(j)], acc_u[:, piece(j)], acc_h[:, piece(j)]
            sig = jax.nn.sigmoid(gate_pre)
            gg[:, piece(j)] = (grad_hidden * up_pre * sig * (1.0 + gate_pre * (1.0 - sig))).astype(BF16)
            ug[:, piece(j)] = (grad_hidden * (gate_pre * sig)).astype(BF16)

        @pl.loop(0, tiles)
        def _(i):
            @pl.when(i + 1 < tiles)
            def _():
                load((0, 1), i + 1)

            loaded((0, 1), i)
            slot = lax.rem(i, 2)
            total = dot_nt(gg[:, piece(0)], buf_g[slot, 0]) + dot_nt(ug[:, piece(0)], buf_u[slot, 0])
            for j in range(1, SLICES):
                total += dot_nt(gg[:, piece(j)], buf_g[slot, j]) + dot_nt(ug[:, piece(j)], buf_u[slot, j])
            ship(1, i, total)

        def picked(target, pick, scale, cols):
            total = dot_nn(pick[0], target[0, :, cols])
            for s in range(1, experts):
                total += dot_nn(pick[s], target[s, :, cols])
            value = total[:token_count] * scale[:, 0:1]
            for n in range(1, top):
                value += total[n * token_count : (n + 1) * token_count] * scale[:, n : n + 1]
            return value

        for copy in token_copies():
            copy.wait()

        @pl.loop(0, tiles)
        def _(i):
            cols = cols_of(i)
            for s in range(experts):
                result_copy(0, i, s).wait()
            next_ref[:, cols] = (tn[:, cols].astype(F32) + picked(recv_o, pn, wn, cols)).astype(BF16)

        def finish(i, mean):
            cols = cols_of(i)
            for s in range(experts):
                result_copy(1, i, s).wait()
            value = picked(recv_g, pp, wp, cols) * gain[:, cols]
            scaled[:, cols] = value
            return mean + jnp.sum(value * tp[:, cols].astype(F32), axis=1, keepdims=True)

        mean = lax.fori_loop(0, tiles, finish, jnp.zeros((token_count, 1), F32)) / width
        inverse = inv[...]
        factor = inverse * inverse * inverse * mean

        @pl.loop(0, tiles)
        def _(i):
            cols = cols_of(i)
            prev_ref[:, cols] = (
                gp[:, cols].astype(F32) + inverse * scaled[:, cols] - tp[:, cols].astype(F32) * factor
            ).astype(BF16)

    three = lambda value: jax.ShapeDtypeStruct((3,) + value.shape, value.dtype)
    in_vmem = pl.BlockSpec(memory_space=pltpu.VMEM)
    result = jax.ShapeDtypeStruct((token_count, width), BF16)
    row_block = pltpu.VMEM((experts, capacity, width), BF16)
    token_block = pltpu.VMEM((token_count, width), BF16)
    wide = (rows, SLICES * ffd)
    dma = pltpu.SemaphoreType.DMA
    return pl.pallas_call(
        kernel,
        in_specs=[ANY] * 7 + [in_vmem] * 6,
        out_specs=[in_vmem] * 2 + [ANY] * 3,
        out_shape=[result] * 2 + [three(gate), three(up), three(down)],
        scratch_shapes=[row_block] * 2
        + [token_block] * 3
        + [row_block] * 2
        + [pltpu.VMEM((token_count, width), F32)]
        + [pltpu.VMEM(wide, F32)] * 3
        + [pltpu.VMEM(wide, BF16)] * 3
        + [pltpu.VMEM((2, SLICES, tile, ffd), BF16)] * 2
        + [pltpu.VMEM((2, SLICES, ffd, tile), BF16)]
        + [dma((3, tiles))] * 4
        + [dma((3,))] * 2
        + [dma((2, tiles, experts - 1))] * 2
        + [dma((3,))] * 2
        + [dma((3, 2, SLICES)), dma((2,))]
        + [dma((2, tiles, experts))] * 2,
        compiler_params=pltpu.CompilerParams(
            collective_id=0, has_side_effects=True, vmem_limit_bytes=VMEM
        ),
        name="layer",
    )(slots_in, slots_grad, gate, up, down, tokens, grad_rows,
      gain_prev, inverse_prev, pick_next, wt_next, pick_prev, wt_prev)[:2]


def slots_of(route_ids, home, experts, capacity):
    token_count, top_count = route_ids.shape
    relative = (route_ids.reshape(-1) - home + experts) % experts
    onehot = (relative[:, None] == jnp.arange(experts, dtype=jnp.int32)[None, :]).astype(jnp.int32)
    before = jnp.cumsum(onehot, axis=0) - onehot
    target = relative * capacity + jnp.sum(before * onehot, axis=1)
    return target.reshape(token_count, top_count)


def pickers_of(pair_slot, experts, capacity):
    flat = pair_slot.T.reshape(-1)
    slots = jnp.arange(experts * capacity, dtype=jnp.int32).reshape(experts, 1, capacity)
    return (flat[None, :, None] == slots).astype(BF16)


def inverse_of(values):
    return lax.rsqrt(jnp.mean(values * values, axis=-1, keepdims=True) + EPSILON)


def body(tokens, grad_out, norm_gain, expert_ids, gate_weights, w_gate, w_up, w_down):
    tokens = tokens[0]
    grad_rows = grad_out[0]
    gain = norm_gain[0][None, :]
    route_ids = expert_ids[0]
    route_weights = gate_weights[0]
    token_count, width = tokens.shape
    top_count = route_ids.shape[1]
    devices = lax.axis_size("expert")
    pipes = lax.axis_size("pipe")
    experts = devices // SLICES
    step_size = 4 * experts * SLICES
    capacity = min(
        token_count, SLICES * ((token_count * top_count * 5 + step_size - 1) // step_size)
    )
    home = lax.axis_index("expert") // SLICES
    same = lambda d: d

    gate, up, down = w_gate[0], w_up[0], w_down[0]

    values = tokens.astype(F32)
    inverse = inverse_of(values)
    normed = (values * inverse * gain).astype(BF16)
    pair_slot = slots_of(route_ids, home, experts, capacity)
    picker = jnp.any(
        pair_slot[None, :, :]
        == jnp.arange(experts * capacity, dtype=jnp.int32)[:, None, None],
        axis=2,
    ).astype(BF16)

    def slotted(rows):
        return dot_nn(picker, rows).astype(BF16).reshape(experts, capacity, width)

    routing = jnp.concatenate([pair_slot.astype(F32), route_weights, inverse], axis=1)
    routing_next = move(routing, 1, same)
    routing_prev = routing_next if pipes == 2 else move(routing, -1, same)
    gain_prev = move(gain, -1, same)

    def routing_of(table):
        slots = table[:, :top_count].astype(jnp.int32)
        return pickers_of(slots, experts, capacity), table[:, top_count : 2 * top_count]

    pick_next, weights_next = routing_of(routing_next)
    pick_prev, weights_prev = routing_of(routing_prev)
    next_rows, prev_rows = layer(
        slotted(normed), slotted(grad_rows), gate, up, down, tokens, grad_rows,
        gain_prev, routing_prev[:, 2 * top_count :],
        pick_next, weights_next, pick_prev, weights_prev,
    )
    return (next_rows[None], prev_rows[None])


def solution(mesh):
    return jax.shard_map(
        body,
        mesh=mesh,
        in_specs=(
            P("pipe", "expert", None),
            P("pipe", "expert", None),
            P("pipe", None),
            P("pipe", "expert", None),
            P("pipe", "expert", None),
            P("pipe", None, "expert"),
            P("pipe", None, "expert"),
            P("pipe", "expert", None),
        ),
        out_specs=(P("pipe", "expert", None), P("pipe", "expert", None)),
        check_vma=False,
    )
```

```python
import jax
import jax.numpy as jnp
from jax import lax
from jax.experimental import pallas as pl
from jax.experimental.pallas import tpu as pltpu
from jax.sharding import PartitionSpec as P

SLICES = 4
EPSILON = 1e-06
BF16 = jnp.bfloat16
F32 = jnp.float32


def move(value, pipe_steps, expert_map):
    pipes, devices = lax.axis_size("pipe"), lax.axis_size("expert")
    pairs = [
        (p * devices + d, ((p + pipe_steps) % pipes) * devices + expert_map(d))
        for p in range(pipes)
        for d in range(devices)
    ]
    return lax.ppermute(value, ("pipe", "expert"), pairs)


def dot_nt(left_arr, right_arr):
    return lax.dot_general(
        left_arr, right_arr, (((1,), (1,)), ((), ())), preferred_element_type=F32
    )


def dot_nn(left_arr, right_arr):
    return jnp.dot(left_arr, right_arr, preferred_element_type=F32)


def tile_of(width):
    for tile in (1024, 512, 256, 128):
        if width % tile == 0:
            return tile
    return width


MESH = pl.DeviceIdType.MESH
ANY = pl.BlockSpec(memory_space=pl.ANY)


def sections():
    pipe, pipes = lax.axis_index("pipe"), lax.axis_size("pipe")
    return pipe, lax.rem(pipe + 1, pipes), lax.rem(pipe + pipes - 1, pipes)


def greet(partners):
    barrier = pltpu.get_barrier_semaphore()
    for partner in partners:
        pl.semaphore_signal(barrier, inc=1, device_id=partner, device_id_type=MESH)
    pl.semaphore_wait(barrier, len(partners))


VMEM = 62 * 1024 * 1024


def layer(picker, inverse, gain, gate, up, down, tokens, grad_rows,
          gain_prev, inverse_prev, pick_next, wt_next, pick_prev, wt_prev):
    rows = picker.shape[0]
    experts, _, capacity = pick_next.shape
    width = tokens.shape[1]
    ffd = down.shape[0]
    token_count, top = wt_next.shape
    devices, pipes = lax.axis_size("expert"), lax.axis_size("pipe")
    tile = tile_of(width)
    tiles = width // tile

    def kernel(pick, inv_own, gain_own, wg, wu, wd, tok, grd, gain, inv, pn, wn, pp, wp,
               next_ref, prev_ref, ag, au, ad,
               ri, rg, si, sg, tn, tp, gp, recv_o, recv_g, scaled, acc_g, acc_u, acc_h, hid, gg, ug,
               buf_g, buf_u, buf_d,
               far_s, far_r, cross_s, cross_r, near_s, near_r, rows_s, rows_r, tok_s, tok_r,
               load_sem, send, recv):
        pipe, after, ahead = sections()
        me = lax.axis_index("expert")
        place = lax.rem(me, SLICES)
        far = me - place + lax.rem(place + 2, SLICES)
        near = me + 1 - 2 * lax.rem(me, 2)
        others = [lax.rem(me + SLICES * s, devices) for s in range(1, experts)]
        homes = [lax.rem(me + devices - SLICES * s, devices) for s in range(experts)]
        greet(
            [(pipe, d) for d in others]
            + [(pipe, far), (pipe, near)]
            + [(p, d) for p in (after, ahead) for d in homes]
        )
        weights = ((wg, ag, buf_g), (wu, au, buf_u), (wd, ad, buf_d))
        stages = (ri, rg)

        def remote(source, target, send_sem, recv_sem, device):
            return pltpu.make_async_remote_copy(
                src_ref=source, dst_ref=target, send_sem=send_sem, recv_sem=recv_sem,
                device_id=device, device_id_type=MESH,
            )

        def cols_of(i):
            return pl.ds(pl.multiple_of(i * tile, tile), tile)

        def part(ref, which, i):
            return ref.at[cols_of(i), :] if which < 2 else ref.at[:, cols_of(i)]

        def far_copy(which, i):
            own, full, _ = weights[which]
            return remote(
                part(own, which, i), part(full.at[1], which, i),
                far_s.at[which, i], far_r.at[which, i], (pipe, far),
            )

        def cross_copy(which, i):
            full = weights[which][1]
            return remote(
                part(full.at[1], which, i), part(full.at[2], which, i),
                cross_s.at[which, i], cross_r.at[which, i], (pipe, near),
            )

        def near_copy(which):
            own, full, _ = weights[which]
            return remote(own, full.at[0], near_s.at[which], near_r.at[which], (pipe, near))

        def row_copy(which, i, s):
            return remote(
                (si, sg)[which].at[s - 1, :, cols_of(i)], stages[which].at[s, :, cols_of(i)],
                rows_s.at[which, i, s - 1], rows_r.at[which, i, s - 1], (pipe, others[s - 1]),
            )

        def token_copies():
            moves = [(tok, tn, after), (grd, gp, ahead), (tok, tp, ahead)]
            return [
                remote(source, target, tok_s.at[n], tok_r.at[n], (device, me))
                for n, (source, target, device) in enumerate(moves)
            ]

        def loads(which, i):
            own, full, buf = weights[which]
            slot = lax.rem(i, 2)
            return [
                pltpu.make_async_copy(
                    part(own if j == 0 else full.at[j - 1], which, i),
                    buf.at[slot, j],
                    load_sem.at[which, slot, j],
                )
                for j in range(SLICES)
            ]

        def load(kinds, i):
            for which in kinds:
                for copy in loads(which, i):
                    copy.start()

        def loaded(kinds, i):
            for which in kinds:
                for copy in loads(which, i):
                    copy.wait()

        def result_copy(which, i, s):
            return remote(
                stages[which].at[s, :, cols_of(i)], (recv_o, recv_g)[which].at[s, :, cols_of(i)],
                send.at[which, i, s], recv.at[which, i, s], ((after, ahead)[which], homes[s]),
            )

        def ship(which, i, total):
            for s in range(experts):
                stages[which][s, :, cols_of(i)] = total[s * capacity : (s + 1) * capacity].astype(BF16)
            for s in range(experts):
                result_copy(which, i, s).start()

        def send_rows(which, i):
            cols = cols_of(i)
            value = tok[:, cols].astype(F32) * inv_own[...] * gain_own[:, cols] if which == 0 else grd[:, cols]
            slots = dot_nn(pick[...], value.astype(BF16))
            stages[which][0, :, cols] = slots[:capacity].astype(BF16)
            for s in range(1, experts):
                (si, sg)[which][s - 1, :, cols] = slots[s * capacity : (s + 1) * capacity].astype(BF16)
            for s in range(experts - 1, 0, -1):
                row_copy(which, i, s).start()

        def send_far(kinds, i):
            for which in kinds:
                far_copy(which, i).start()

        def tile_rows(which, i):
            return stages[which][:, :, cols_of(i)].reshape(rows, tile)

        def piece(j):
            return slice(j * ffd, (j + 1) * ffd)

        first_far, first_down = min(2, tiles), min(4, tiles)
        for i in range(first_far):
            send_far((0, 1), i)

        @pl.loop(0, tiles)
        def _(i):
            send_rows(0, i)

        for which in range(3):
            near_copy(which).start()
        for copy in token_copies():
            copy.start()
        acc_g[...] = jnp.zeros_like(acc_g)
        acc_u[...] = jnp.zeros_like(acc_u)
        acc_h[...] = jnp.zeros_like(acc_h)
        near_copy(0).wait()
        near_copy(1).wait()

        def pipeline(kinds, arrive, compute):
            @pl.loop(0, tiles + 2)
            def _(i):
                @pl.when(i < tiles)
                def _():
                    arrive(i)
                    for which in kinds:
                        far_copy(which, i).wait()
                        cross_copy(which, i).start()

                @pl.when((i >= 1) & (i <= tiles))
                def _():
                    for which in kinds:
                        cross_copy(which, i - 1).wait()
                    load(kinds, i - 1)

                @pl.when(i >= 2)
                def _():
                    loaded(kinds, i - 2)
                    compute(i - 2)

        def arrive_first(i):
            send_rows(1, i)

            @pl.when(i + first_far < tiles)
            def _():
                send_far((0, 1), i + first_far)

            @pl.when(i == tiles - 1)
            def _():
                for n in range(first_down):
                    send_far((2,), n)

        def compute_first(i):
            for s in range(1, experts):
                row_copy(0, i, s).wait()
            slot = lax.rem(i, 2)
            block = tile_rows(0, i)
            for j in range(SLICES):
                acc_g[:, piece(j)] += dot_nn(block, buf_g[slot, j])
                acc_u[:, piece(j)] += dot_nn(block, buf_u[slot, j])

        pipeline((0, 1), arrive_first, compute_first)

        for j in range(SLICES):
            gate_pre = acc_g[:, piece(j)]
            hid[:, piece(j)] = (gate_pre * jax.nn.sigmoid(gate_pre) * acc_u[:, piece(j)]).astype(BF16)
        near_copy(2).wait()

        def arrive_down(i):
            @pl.when(i + first_down < tiles)
            def _():
                send_far((2,), i + first_down)

        def compute_down(i):
            slot = lax.rem(i, 2)
            total = dot_nn(hid[:, piece(0)], buf_d[slot, 0])
            for j in range(1, SLICES):
                total += dot_nn(hid[:, piece(j)], buf_d[slot, j])
            ship(0, i, total)
            for s in range(1, experts):
                row_copy(1, i, s).wait()
            block = tile_rows(1, i)
            for j in range(SLICES):
                acc_h[:, piece(j)] += dot_nt(block, buf_d[slot, j])

        pipeline((2,), arrive_down, compute_down)

        load((0, 1), 0)
        for j in range(SLICES):
            gate_pre, up_pre, grad_hidden = acc_g[:, piece(j)], acc_u[:, piece(j)], acc_h[:, piece(j)]
            sig = jax.nn.sigmoid(gate_pre)
            gg[:, piece(j)] = (grad_hidden * up_pre * sig * (1.0 + gate_pre * (1.0 - sig))).astype(BF16)
            ug[:, piece(j)] = (grad_hidden * (gate_pre * sig)).astype(BF16)

        @pl.loop(0, tiles)
        def _(i):
            @pl.when(i + 1 < tiles)
            def _():
                load((0, 1), i + 1)

            loaded((0, 1), i)
            slot = lax.rem(i, 2)
            total = dot_nt(gg[:, piece(0)], buf_g[slot, 0]) + dot_nt(ug[:, piece(0)], buf_u[slot, 0])
            for j in range(1, SLICES):
                total += dot_nt(gg[:, piece(j)], buf_g[slot, j]) + dot_nt(ug[:, piece(j)], buf_u[slot, j])
            ship(1, i, total)

        def picked(target, pick, scale, cols):
            total = dot_nn(pick[0], target[0, :, cols])
            for s in range(1, experts):
                total += dot_nn(pick[s], target[s, :, cols])
            value = total[:token_count] * scale[:, 0:1]
            for n in range(1, top):
                value += total[n * token_count : (n + 1) * token_count] * scale[:, n : n + 1]
            return value

        for copy in token_copies():
            copy.wait()

        @pl.loop(0, tiles)
        def _(i):
            cols = cols_of(i)
            for s in range(experts):
                result_copy(0, i, s).wait()
            next_ref[:, cols] = (tn[:, cols].astype(F32) + picked(recv_o, pn, wn, cols)).astype(BF16)

        def finish(i, mean):
            cols = cols_of(i)
            for s in range(experts):
                result_copy(1, i, s).wait()
            value = picked(recv_g, pp, wp, cols) * gain[:, cols]
            scaled[:, cols] = value
            return mean + jnp.sum(value * tp[:, cols].astype(F32), axis=1, keepdims=True)

        mean = lax.fori_loop(0, tiles, finish, jnp.zeros((token_count, 1), F32)) / width
        inverse = inv[...]
        factor = inverse * inverse * inverse * mean

        @pl.loop(0, tiles)
        def _(i):
            cols = cols_of(i)
            prev_ref[:, cols] = (
                gp[:, cols].astype(F32) + inverse * scaled[:, cols] - tp[:, cols].astype(F32) * factor
            ).astype(BF16)

    three = lambda value: jax.ShapeDtypeStruct((3,) + value.shape, value.dtype)
    in_vmem = pl.BlockSpec(memory_space=pltpu.VMEM)
    result = jax.ShapeDtypeStruct((token_count, width), BF16)
    row_block = pltpu.VMEM((experts, capacity, width), BF16)
    token_block = pltpu.VMEM((token_count, width), BF16)
    wide = (rows, SLICES * ffd)
    dma = pltpu.SemaphoreType.DMA
    return pl.pallas_call(
        kernel,
        in_specs=[in_vmem] * 3 + [ANY] * 3 + [in_vmem] * 8,
        out_specs=[in_vmem] * 2 + [ANY] * 3,
        out_shape=[result] * 2 + [three(gate), three(up), three(down)],
        scratch_shapes=[row_block] * 2
        + [pltpu.VMEM((experts - 1, capacity, width), BF16)] * 2
        + [token_block] * 3
        + [row_block] * 2
        + [pltpu.VMEM((token_count, width), F32)]
        + [pltpu.VMEM(wide, F32)] * 3
        + [pltpu.VMEM(wide, BF16)] * 3
        + [pltpu.VMEM((2, SLICES, tile, ffd), BF16)] * 2
        + [pltpu.VMEM((2, SLICES, ffd, tile), BF16)]
        + [dma((3, tiles))] * 4
        + [dma((3,))] * 2
        + [dma((2, tiles, experts - 1))] * 2
        + [dma((3,))] * 2
        + [dma((3, 2, SLICES))]
        + [dma((2, tiles, experts))] * 2,
        compiler_params=pltpu.CompilerParams(
            collective_id=0, has_side_effects=True, vmem_limit_bytes=VMEM
        ),
        name="layer",
    )(picker, inverse, gain, gate, up, down, tokens, grad_rows,
      gain_prev, inverse_prev, pick_next, wt_next, pick_prev, wt_prev)[:2]


def slots_of(route_ids, home, experts, capacity):
    token_count, top_count = route_ids.shape
    relative = (route_ids.reshape(-1) - home + experts) % experts
    onehot = (relative[:, None] == jnp.arange(experts, dtype=jnp.int32)[None, :]).astype(jnp.int32)
    before = jnp.cumsum(onehot, axis=0) - onehot
    target = relative * capacity + jnp.sum(before * onehot, axis=1)
    return target.reshape(token_count, top_count)


def pickers_of(pair_slot, experts, capacity):
    flat = pair_slot.T.reshape(-1)
    slots = jnp.arange(experts * capacity, dtype=jnp.int32).reshape(experts, 1, capacity)
    return (flat[None, :, None] == slots).astype(BF16)


def inverse_of(values):
    return lax.rsqrt(jnp.mean(values * values, axis=-1, keepdims=True) + EPSILON)


def body(tokens, grad_out, norm_gain, expert_ids, gate_weights, w_gate, w_up, w_down):
    tokens = tokens[0]
    grad_rows = grad_out[0]
    gain = norm_gain[0][None, :]
    route_ids = expert_ids[0]
    route_weights = gate_weights[0]
    token_count, width = tokens.shape
    top_count = route_ids.shape[1]
    devices = lax.axis_size("expert")
    pipes = lax.axis_size("pipe")
    experts = devices // SLICES
    step_size = 4 * experts * SLICES
    capacity = min(
        token_count, SLICES * ((token_count * top_count * 5 + step_size - 1) // step_size)
    )
    home = lax.axis_index("expert") // SLICES
    same = lambda d: d

    gate, up, down = w_gate[0], w_up[0], w_down[0]

    values = tokens.astype(F32)
    inverse = inverse_of(values)
    pair_slot = slots_of(route_ids, home, experts, capacity)
    picker = jnp.any(
        pair_slot[None, :, :]
        == jnp.arange(experts * capacity, dtype=jnp.int32)[:, None, None],
        axis=2,
    ).astype(BF16)

    routing = jnp.concatenate([pair_slot.astype(F32), route_weights, inverse], axis=1)
    routing_next = move(routing, 1, same)
    routing_prev = routing_next if pipes == 2 else move(routing, -1, same)
    gain_prev = move(gain, -1, same)

    def routing_of(table):
        slots = table[:, :top_count].astype(jnp.int32)
        return pickers_of(slots, experts, capacity), table[:, top_count : 2 * top_count]

    pick_next, weights_next = routing_of(routing_next)
    pick_prev, weights_prev = routing_of(routing_prev)
    next_rows, prev_rows = layer(
        picker, inverse, gain, gate, up, down, tokens, grad_rows,
        gain_prev, routing_prev[:, 2 * top_count :],
        pick_next, weights_next, pick_prev, weights_prev,
    )
    return (next_rows[None], prev_rows[None])


def solution(mesh):
    return jax.shard_map(
        body,
        mesh=mesh,
        in_specs=(
            P("pipe", "expert", None),
            P("pipe", "expert", None),
            P("pipe", None),
            P("pipe", "expert", None),
            P("pipe", "expert", None),
            P("pipe", None, "expert"),
            P("pipe", None, "expert"),
            P("pipe", "expert", None),
        ),
        out_specs=(P("pipe", "expert", None), P("pipe", "expert", None)),
        check_vma=False,
    )
```
